256 devices in a mesh: dp: 2 (over core), ctx: 128 (over y, z, x).
Axes of the slice: x: 4, y: 4, z: 8, core: 2. Of those that a mesh axis runs over, the one named last changes fastest.
Arguments:
- queries: bfloat16 [32768, 1024], P(('dp', 'ctx')), parts along dimension 0, may hold values from -6 to 6
- keys: bfloat16 [32768, 1024], P(('dp', 'ctx')), parts along dimension 0, may hold values from -6 to 6
- values: bfloat16 [32768, 1024], P(('dp', 'ctx')), parts along dimension 0, may hold values from -7.5 to 7.5
- hidden: bfloat16 [32768, 1024], P(('dp', 'ctx')), parts along dimension 0, may hold values from -60 to 60
- out_weight: bfloat16 [1024, 1024], replicated, may hold values from -0.1875 to 0.1875
- norm_gain: float32 [1024], replicated, may hold values from 0.1 to 1.9
- random_blocks: int32 [512, 16, 3], P('dp'), parts along dimension 0, may hold values from 0 to 255, as said below
- global_blocks: int32 [4], P('dp'), parts along dimension 0, may hold values from 0 to 255, as said below
Outputs:
- normed: bfloat16 [32768, 1024], P(('dp', 'ctx')), parts along dimension 0
The draws below stay inside these ranges and needn't reach their ends.
There are 2 independent parts, one for each index of `dp`. The reference program is written for one: setup_inputs(seed, part) draws one part's arguments, and reference() takes and returns one part's arrays. A program takes and returns all parts, laid end to end along the dimension named above; an argument that names none is the same for every part. Nothing has to cross between parts.
Inputs may be any that keep to these rules, and one draw needn't show every extreme that they name: `random_blocks`: among the random blocks named by the query blocks of one index of ctx (rows d * 2 to (d + 1) * 2 - 1, all heads), at most 2 lie in the blocks of any one index of ctx (block // 2); for every d some index is named exactly 2 times. `global_blocks`: the 2 global blocks are distinct, and one of them is the last block of the document.
All inputs are finite; a program needn't handle non-finite values.
Results may differ from the reference program's by a relative error of at most 0.001.
The reference program's roundings to bfloat16 on the way (of `probabilities` and `attended`) count: a program that leaves them out, or rounds other values in their place, can miss the bound.
Values may be sent and summed in bfloat16 or wider, within the bound.
A program may use at most 64 MiB of HBM per device.

```python
import math
import jax
import jax.numpy as jnp
from jax import lax

D = 1024
H = 16
BLOCK = 64
R = 3
G = 2
REACH = 1
TOK_DEV = 128
HD = 64
BPD = 2
NBLK = 256
TOKENS = 16384
REQ = 96
CAP = 2
N_CTX = 128


def paired_fields(key):
    base_key = jax.random.fold_in(key, 7)
    key_one, key_two = jax.random.split(base_key, 2)
    query_field = jnp.clip(jax.random.normal(key_one, (TOKENS, D), jnp.float32), -6.0, 6.0)
    key_field = jnp.clip(jax.random.normal(key_two, (TOKENS, D), jnp.float32), -6.0, 6.0)
    return (query_field, key_field)


def draw_queries(key, part):
    return paired_fields(key)[0].astype(jnp.bfloat16)


def draw_keys(key, part):
    return paired_fields(key)[1].astype(jnp.bfloat16)


def draw_values(key, part):
    key_one, key_two = jax.random.split(jax.random.fold_in(key, 5), 2)
    device_total = TOKENS // TOK_DEV
    sample_field = jnp.clip(jax.random.normal(key_one, (TOKENS, D), jnp.float32), -5.0, 5.0)
    offset_field = jax.random.uniform(key_two, (device_total, 1, D), jnp.float32, -2.5, 2.5)
    return (sample_field.reshape(device_total, TOK_DEV, D) + offset_field).reshape(TOKENS, D).astype(jnp.bfloat16)


def draw_hidden(key, part):
    key_one = jax.random.fold_in(jax.random.fold_in(key, 3), 0)
    sample_field = jnp.clip(jax.random.normal(key_one, (TOKENS, D), jnp.float32), -6.0, 6.0)
    return sample_field.astype(jnp.bfloat16)


def draw_random_blocks(key, part):
    device_total = TOKENS // TOK_DEV
    slot_total = device_total * CAP

    def one_device(sub_key):
        key_one, key_two, key_three, key_four = jax.random.split(sub_key, 4)
        forced = jax.random.randint(key_one, (), 0, device_total, jnp.int32)
        slot_ids = jnp.arange(slot_total, dtype=jnp.int32)
        noise_bits = jax.random.randint(key_two, (slot_total,), 0, 1 << 20, jnp.int32)
        slot_score = noise_bits * slot_total + slot_ids
        slot_score = jnp.where(slot_ids // CAP == forced, slot_ids - slot_total, slot_score)
        slot_order = jnp.argsort(slot_score, stable=True).astype(jnp.int32)
        owner_ids = slot_order[:REQ] // CAP
        owner_ids = jax.random.permutation(key_three, owner_ids)
        inner_block = jax.random.randint(key_four, (REQ,), 0, BPD, jnp.int32)
        return (owner_ids * BPD + inner_block).astype(jnp.int32)
    device_keys = jax.random.split(jax.random.fold_in(key, 9), device_total)
    return jax.vmap(one_device)(device_keys).reshape(NBLK, H, R)


def draw_global_blocks(key, part):
    key_one, key_two = jax.random.split(jax.random.fold_in(key, 17), 2)
    block_total = TOKENS // BLOCK
    others = jax.random.permutation(key_one, block_total - 1)[:G - 1].astype(jnp.int32)
    chosen = jnp.concatenate([jnp.full((1,), block_total - 1, jnp.int32), others])
    return jax.random.permutation(key_two, chosen).astype(jnp.int32)


def noise(own_key, dims, scale, most, kind=jnp.bfloat16):
    result = jax.random.normal(own_key, dims, jnp.float32) * scale
    return jnp.minimum(jnp.maximum(result, -most), most).astype(kind)


def setup_inputs(seed: int = 0, part: int = 0) -> dict:
    splits = jax.random.split(jax.random.key(seed), 9)
    part_keys = jax.random.split(jax.random.fold_in(splits[8], part), 9)
    queries = draw_queries(jax.random.fold_in(jax.random.fold_in(splits[8], part), 71), part)
    keys = draw_keys(jax.random.fold_in(jax.random.fold_in(splits[8], part), 71), part)
    values = draw_values(jax.random.fold_in(jax.random.fold_in(splits[8], part), 71), part)
    hidden = draw_hidden(jax.random.fold_in(jax.random.fold_in(splits[8], part), 71), part)
    out_weight = noise(splits[4], (D, D), D ** -0.5, 0.1875)
    norm_gain = jnp.clip(1.0 + 0.18 * jax.random.normal(splits[5], (D,), jnp.float32), 0.1, 1.9)
    random_blocks = draw_random_blocks(jax.random.fold_in(jax.random.fold_in(splits[8], part), 71), part)
    global_blocks = draw_global_blocks(jax.random.fold_in(jax.random.fold_in(splits[8], part), 71), part)
    return dict(queries=queries, keys=keys, values=values, hidden=hidden, out_weight=out_weight, norm_gain=norm_gain, random_blocks=random_blocks, global_blocks=global_blocks)


def reference(queries, keys, values, hidden, out_weight, norm_gain, random_blocks, global_blocks):
    score_scale = 1.0 / math.sqrt(HD)
    window_span = 2 * REACH + 1
    key_heads = keys.reshape(TOKENS, H, HD)
    value_heads = values.reshape(TOKENS, H, HD)
    kv_rows = jnp.concatenate([key_heads, value_heads], axis=2)
    kv_blocks = kv_rows.reshape(NBLK, BLOCK, H, 2 * HD)
    padded = jnp.pad(kv_blocks, ((REACH, REACH), (0, 0), (0, 0), (0, 0)))
    query_blocks = queries.reshape(NBLK, BLOCK, H, HD)
    global_kv = kv_blocks[global_blocks].reshape(G * BLOCK, H, 2 * HD).astype(jnp.float32)
    head_index = jnp.arange(H, dtype=jnp.int32)
    offsets = jnp.arange(window_span, dtype=jnp.int32) - REACH

    def group_context(block_start):
        q_group = lax.dynamic_slice_in_dim(query_blocks, block_start, BPD, 0).astype(jnp.float32)
        window = jnp.stack([lax.dynamic_slice_in_dim(padded, block_start + shift_index, BPD, 0) for shift_index in range(window_span)], axis=1).astype(jnp.float32)
        chosen = lax.dynamic_slice_in_dim(random_blocks, block_start, BPD, 0)
        remote = kv_blocks[chosen, :, head_index[None, :, None], :].astype(jnp.float32)
        block_ids = block_start + jnp.arange(BPD, dtype=jnp.int32)
        target = block_ids[:, None] + offsets[None, :]
        allowed = (target >= 0) & (target < NBLK)
        s_window = jnp.einsum('bqhd,bwkhd->bhqwk', q_group, window[..., :HD]) * score_scale
        s_window = jnp.where(allowed[:, None, None, :, None], s_window, -1e+30)
        s_global = jnp.einsum('bqhd,khd->bhqk', q_group, global_kv[..., :HD]) * score_scale
        s_random = jnp.einsum('bqhd,bhrkd->bhqrk', q_group, remote[..., :HD]) * score_scale
        all_scores = jnp.concatenate([s_window.reshape(BPD, H, BLOCK, window_span * BLOCK), s_global, s_random.reshape(BPD, H, BLOCK, R * BLOCK)], axis=3)
        rounded = jax.nn.softmax(all_scores, axis=3).astype(jnp.bfloat16)
        probabilities = lax.optimization_barrier(rounded).astype(jnp.float32)
        window_probs = probabilities[..., :window_span * BLOCK].reshape(BPD, H, BLOCK, window_span, BLOCK)
        global_probs = probabilities[..., window_span * BLOCK:(window_span + G) * BLOCK]
        random_probs = probabilities[..., (window_span + G) * BLOCK:].reshape(BPD, H, BLOCK, R, BLOCK)
        context_part = jnp.einsum('bhqwk,bwkhd->bqhd', window_probs, window[..., HD:])
        context_part = context_part + jnp.einsum('bhqk,khd->bqhd', global_probs, global_kv[..., HD:])
        context_part = context_part + jnp.einsum('bhqrk,bhrkd->bqhd', random_probs, remote[..., HD:])
        return context_part
    starts = jnp.arange(N_CTX, dtype=jnp.int32) * BPD
    context = lax.map(group_context, starts).reshape(NBLK, BLOCK, H, HD)
    global_queries = query_blocks[global_blocks].reshape(G * BLOCK, H, HD)

    def head_context(head):
        query_head = global_queries[:, head, :]
        key_head = key_heads[:, head, :]
        value_head = value_heads[:, head, :].astype(jnp.float32)
        head_scores = jnp.dot(query_head, key_head.T, preferred_element_type=jnp.float32) * score_scale
        weights = jnp.exp(head_scores - lax.optimization_barrier(jnp.max(head_scores, axis=1, keepdims=True)))
        numer = jnp.dot(weights, value_head, precision=lax.Precision.HIGHEST)
        return numer / lax.optimization_barrier(jnp.sum(weights, axis=1, keepdims=True))
    global_context = lax.map(head_context, head_index)
    global_context = jnp.transpose(global_context, (1, 0, 2)).reshape(G, BLOCK, H, HD)
    context = context.at[global_blocks].set(global_context)
    attended = context.reshape(TOKENS, D).astype(jnp.bfloat16)
    mixed_rows = hidden.astype(jnp.float32) + jnp.dot(attended, out_weight, preferred_element_type=jnp.float32)
    row_mean = lax.optimization_barrier(jnp.mean(mixed_rows, axis=1, keepdims=True))
    centred = mixed_rows - row_mean
    variance = lax.optimization_barrier(jnp.mean(centred * centred, axis=1, keepdims=True))
    return (centred * lax.rsqrt(variance + 1e-05) * norm_gain[None, :]).astype(jnp.bfloat16)
```

```python
import functools
import math

import jax
import jax.numpy as jnp
from jax import lax
from jax.experimental import pallas as pl
from jax.experimental.pallas import tpu as pltpu
from jax.sharding import PartitionSpec as P

BLOCK = 64
G = 2
NX, NY, NZ = 4, 4, 8
BATCHES = (10, 10, 10, 20, 12, 10, 14)
MESH = pl.DeviceIdType.MESH
bf16 = jnp.bfloat16
f32 = jnp.float32


def swap_halves(x):
    return jnp.concatenate([x[:, 64:], x[:, :64]], axis=1)


def low_half(shape):
    return lax.broadcasted_iota(jnp.int32, shape, 1) < 64


def prep_kernel(heads, rand, queries, keys, values, rb, gb, payload, kvt, qt, candq, candkv, rtab,
                tab_v, tab_s, rb_s, seen, sem):
    count = NX * NY * NZ
    me = lax.axis_index("ctx")
    pairs = heads // 2
    copy_rb = pltpu.make_async_copy(rb, rb_s, sem.at[0])
    copy_rb.start()
    lanes = 2 * count
    first = jnp.full((1, lanes), 1e9, f32)
    last = jnp.full((1, lanes), -1.0, f32)
    lane = lax.broadcasted_iota(jnp.int32, (heads, lanes), 1)
    head = lax.broadcasted_iota(jnp.int32, (heads, lanes), 0)
    for r in range(rand):
        req = rb[r]
        mine = (req // 2) == me
        key = (((lane % 2) * heads + head) * rand + r) * 2 + req % 2
        key = key.astype(f32)
        first = jnp.minimum(first, jnp.min(jnp.where(mine, key, 1e9), axis=0, keepdims=True))
        last = jnp.maximum(last, jnp.max(jnp.where(mine, key, -1.0), axis=0, keepdims=True))
    first = jnp.minimum(first, pltpu.roll(first, lanes - 1, 1))
    last = jnp.maximum(last, pltpu.roll(last, lanes - 1, 1))

    def to_tile(key):
        key = jnp.clip(key, 0.0, float(4 * heads * rand - 1)).astype(jnp.int32)
        return (key % 2) * heads + (key // 2 // rand) % heads

    tab_v[0:1, :] = to_tile(first)
    tab_v[1:2, :] = to_tile(last)
    copy_tab = pltpu.make_async_copy(tab_v, tab_s, sem.at[1])
    copy_tab.start()
    low = low_half((BLOCK, 128))
    zero = jnp.zeros((BLOCK, 128), bf16)
    for b in range(2):
        rows = slice(b * BLOCK, (b + 1) * BLOCK)
        for p in range(pairs):
            cols = slice(p * 128, (p + 1) * 128)
            kr = swap_halves(keys[rows, cols])
            vn = values[rows, cols]
            qr = swap_halves(queries[rows, cols])
            kvt[b * heads + 2 * p] = jnp.where(low, vn, kr)
            kvt[b * heads + 2 * p + 1] = jnp.where(low, kr, vn)
            qt[2 * p, rows, :] = jnp.where(low, zero, qr)
            qt[2 * p + 1, rows, :] = jnp.where(low, qr, zero)
    for g in range(G):
        local = gb[g] % 2

        def pick(h, c):
            candkv[h, g] = kvt[local * heads + h]
            return c

        lax.fori_loop(0, heads, pick, 0)
        for p in range(pairs):
            candq[g * pairs + p] = queries[pl.ds(pl.multiple_of(local * BLOCK, BLOCK), BLOCK), p * 128:(p + 1) * 128]

    def clear(i, c):
        seen[i] = 0
        return c

    lax.fori_loop(0, count, clear, 0)
    copy_rb.wait()

    def mark(i, c):
        b = i // (heads * rand)
        h = (i // rand) % heads
        owner = rb_s[i % rand, h, 2 * me + b] // 2
        slot = seen[owner]
        rtab[i] = owner * 2 + slot
        seen[owner] = 1
        return c

    lax.fori_loop(0, 2 * heads * rand, mark, 0)
    copy_tab.wait()

    def fill(d, c):
        payload[2 * d] = kvt[tab_s[0, 2 * d]]
        payload[2 * d + 1] = kvt[tab_s[1, 2 * d]]
        return c

    lax.fori_loop(0, count, fill, 0)


def main_kernel(heads, rand, payload, kvt, qt, candq, candkv, hidden, weight, gain, gb, rtab, out,
                recv, win, recvq, zq, gq, recvkv, zkv, gkv, part, rpart, zpart, ghead, gctx, att,
                a2a_s, a2a_r, send, got, loc):
    count, plane = NX * NY * NZ, NX * NY
    pairs = heads // 2
    zrows = 2 * BLOCK // NZ
    me = lax.axis_index("ctx")
    x, z, y = me % NX, (me // NX) % NZ, me // (NX * NZ)
    pos = y * NX + x

    def at(px, pz, py):
        return {"ctx": (py * NZ + pz) * NX + px}

    def shifted(k):
        kx, kz, ky = k % NX, (k // NX) % NZ, k // (NX * NZ)
        return ((y + ky) % NY * NZ + (z + kz) % NZ) * NX + (x + kx) % NX

    def remote(src, dst, s, r, device):
        return pltpu.make_async_remote_copy(
            src_ref=src, dst_ref=dst, send_sem=s, recv_sem=r, device_id=device, device_id_type=MESH)

    barrier = pltpu.get_barrier_semaphore()

    def greet(k, c):
        pl.semaphore_signal(barrier, inc=1, device_id={"ctx": shifted(k)}, device_id_type=MESH)
        return c

    lax.fori_loop(1, count, greet, 0)
    pl.semaphore_wait(barrier, count - 1)

    issued = [1]

    def batch(n):
        lo = issued[0]
        hi = min(count, lo + n)
        issued[0] = hi

        def one(k, c):
            d = shifted((k * 37) % count)
            remote(payload.at[pl.ds(2 * d, 2)], recv.at[pl.ds(2 * me, 2)], a2a_s, a2a_r, {"ctx": d}).start()
            return c

        if hi > lo:
            lax.fori_loop(lo, hi, one, 0)

    def to_plane(fn, i):
        def one(k, c):
            p = ((y + k // NX) % NY) * NX + (x + k % NX) % NX
            src, dst = fn(p)
            remote(src, dst, send.at[i], got.at[i], at(p % NX, z, p // NX)).start()
            return c

        lax.fori_loop(1, plane, one, 0)

    def to_line(fn, i):
        def one(k, c):
            pz = (z + k) % NZ
            src, dst = fn(pz)
            remote(src, dst, send.at[i], got.at[i], at(x, pz, y)).start()
            return c

        lax.fori_loop(1, NZ, one, 0)

    def wait_got(ref, i):
        pltpu.make_async_copy(ref, ref, got.at[i]).wait()

    def wait_sent(ref, i):
        pltpu.make_async_copy(ref, ref, send.at[i]).wait()

    def owner_of(g):
        return gb[g] // 2

    def pos_of(d):
        return (d // (NX * NZ)) * NX + d % NX

    def z_of(d):
        return (d // NX) % NZ

    own = [
        pltpu.make_async_copy(candq.at[pos], recvq.at[pos], loc.at[0]),
        pltpu.make_async_copy(candkv.at[pos], recvkv.at[pos], loc.at[1]),
        pltpu.make_async_copy(payload.at[pl.ds(2 * me, 2)], recv.at[pl.ds(2 * me, 2)], loc.at[2]),
    ]
    for c in own:
        c.start()

    to_plane(lambda p: (candq.at[p], recvq.at[pos]), 0)
    to_plane(lambda p: (candkv.at[p], recvkv.at[pos]), 1)
    batch(BATCHES[0])
    own[0].wait()
    wait_got(recvq.at[pl.ds(0, plane - 1)], 0)
    my_g = pos // pairs
    q_owner = owner_of(my_g)
    zq[z] = recvq[pos_of(q_owner)]
    batch(2)
    to_line(lambda p: (zq.at[z], zq.at[z]), 2)
    batch(BATCHES[1] - 2)
    own[1].wait()
    wait_got(recvkv.at[pl.ds(0, plane - 1)], 1)
    for g in range(G):
        zkv[z, g] = recvkv[pos_of(owner_of(g)), g]
    wait_got(zq.at[pl.ds(0, NZ - 1)], 2)
    gq[pos] = zq[z_of(q_owner)]
    batch(2)
    to_plane(lambda p: (gq.at[pos], gq.at[pos]), 3)
    to_line(lambda p: (zkv.at[z], zkv.at[z]), 4)
    nxt, prv = (me + 1) % count, (me + count - 1) % count
    w0 = remote(kvt.at[pl.ds(heads, heads)], win.at[0], send.at[5], got.at[5], {"ctx": nxt})
    w1 = remote(kvt.at[pl.ds(0, heads)], win.at[1], send.at[6], got.at[6], {"ctx": prv})
    batch(BATCHES[2] - 2)
    wait_got(gq.at[pl.ds(0, plane - 1)], 3)

    lane = lax.broadcasted_iota(jnp.int32, (2 * BLOCK, 128), 1)
    low = lane < 64

    def score(q, tiles):
        return lax.dot_general(q, tiles, (((1,), (1,)), ((), ())), preferred_element_type=f32) * 0.125

    def send_part(h):
        @pl.when(h != pos)
        def _():
            remote(part.at[h], rpart.at[pos], send.at[7], got.at[7], at(h % NX, z, h // NX)).start()

    per_pair = max(1, BATCHES[3] // pairs)

    def partial(i, c):
        @pl.when(i > 0)
        def _():
            before = (pos // 2 + i) % pairs
            send_part(2 * before)
            send_part(2 * before + 1)

        p = (pos // 2 + i + 1) % pairs
        q = jnp.concatenate([gq[p], gq[pairs + p]], axis=0)
        q = swap_halves(q)
        for odd in range(2):
            h = 2 * p + odd
            tiles = jnp.concatenate([kvt[h], kvt[heads + h]], axis=0)
            mine = low if odd else jnp.logical_not(low)
            s = score(jnp.where(mine, q, jnp.zeros_like(q)), tiles)
            top = jnp.max(s, axis=1, keepdims=True)
            e = jnp.exp(s - top)
            total = jnp.sum(e, axis=1, keepdims=True)
            hi = e.astype(bf16)
            lo = (e - hi.astype(f32)).astype(bf16)
            numer = jnp.dot(hi, tiles, preferred_element_type=f32) + jnp.dot(lo, tiles, preferred_element_type=f32)
            stats = jnp.where(lane % 64 < 32, total, top)
            part[h] = jnp.where(mine, stats, numer)
        return c

    lax.fori_loop(0, pairs, partial, 0)
    batch(2)
    last_pair = pos // 2
    send_part(2 * last_pair)
    send_part(2 * last_pair + 1)
    own_part = pltpu.make_async_copy(part.at[pos], rpart.at[pos], loc.at[3])
    own_part.start()
    batch(BATCHES[3])
    w0.start()
    w1.start()
    wait_got(zkv.at[pl.ds(0, NZ - 1)], 4)
    for g in range(G):
        gkv[pos, g] = zkv[z_of(owner_of(g)), g]
    batch(2)
    to_plane(lambda p: (gkv.at[pos], gkv.at[pos]), 8)

    odd_head = pos % 2 == 1

    def merge(ref, n, rows):
        ln = lax.broadcasted_iota(jnp.int32, (rows, 128), 1)
        stat = (ln < 64) == odd_head
        is_top = jnp.logical_and(stat, ln % 64 >= 32)
        tops = [jnp.max(jnp.where(is_top, ref[j], -3e38), axis=1, keepdims=True) for j in range(n)]
        top = functools.reduce(jnp.maximum, tops)
        acc = functools.reduce(jnp.add, [ref[j] * jnp.exp(tops[j] - top) for j in range(n)])
        is_total = jnp.logical_and(stat, ln % 64 < 32)
        total = jnp.max(jnp.where(is_total, acc, 0.0), axis=1, keepdims=True)
        return jnp.where(is_top, top, acc), total

    own_part.wait()
    wait_got(rpart.at[pl.ds(0, plane - 1)], 7)

    def merge_rows(i, c):
        rows = pl.ds(pl.multiple_of(i * zrows, zrows), zrows)
        merged, _ = merge(rpart.at[:, rows, :], plane, zrows)
        zsum_ref = part.at[0]
        zsum_ref[rows, :] = merged
        return c

    wait_sent(part.at[pl.ds(0, plane - 1)], 7)
    lax.fori_loop(0, NZ, merge_rows, 0)
    own_z = pltpu.make_async_copy(
        part.at[0, pl.ds(pl.multiple_of(z * zrows, zrows), zrows)], zpart.at[z], loc.at[4])
    batch(2)
    to_line(lambda p: (part.at[0, pl.ds(pl.multiple_of(p * zrows, zrows), zrows)], zpart.at[z]), 9)
    own_z.start()
    batch(BATCHES[4] - 2)
    own_z.wait()
    wait_got(zpart.at[pl.ds(0, NZ - 1)], 9)
    acc, total = merge(zpart, NZ, zrows)
    my_rows = pl.ds(pl.multiple_of(z * zrows, zrows), zrows)
    ghead[z] = (acc / total).astype(bf16)
    batch(2)
    to_line(lambda p: (ghead.at[z], ghead.at[z]), 10)
    batch(BATCHES[5] - 2)
    wait_got(ghead.at[pl.ds(0, NZ - 1)], 10)
    own_g = pltpu.make_async_copy(ghead, gctx.at[pos], loc.at[5])
    own_g.start()
    to_plane(lambda p: (ghead, gctx.at[pos]), 11)
    batch(BATCHES[6])
    batch(count)
    own_g.wait()
    own[2].wait()
    wait_got(gctx.at[pl.ds(0, plane - 1)], 11)
    wait_got(gkv.at[pl.ds(0, plane - 1)], 8)
    w0.wait_recv()
    w1.wait_recv()
    pltpu.make_async_copy(recv.at[pl.ds(0, 2 * count - 2)], recv.at[pl.ds(0, 2 * count - 2)], a2a_r).wait()

    row = lax.broadcasted_iota(jnp.int32, (2 * BLOCK, 6 * BLOCK), 0)
    col = lax.broadcasted_iota(jnp.int32, (2 * BLOCK, 6 * BLOCK), 1)
    first_rows = row < BLOCK
    is_prev = col < BLOCK
    is_next = jnp.logical_and(col >= 3 * BLOCK, col < 4 * BLOCK)
    no_prev = jnp.logical_or(jnp.logical_not(first_rows), me == 0)
    no_next = jnp.logical_or(first_rows, me == count - 1)
    hidden_keys = jnp.logical_or(jnp.logical_and(is_prev, no_prev), jnp.logical_and(is_next, no_next))
    low_b = low_half((BLOCK, 128))

    def attend(p, c):
        results = []
        for odd in range(2):
            h = 2 * p + odd
            tiles = jnp.concatenate(
                [win[0, h], kvt[h], kvt[heads + h], win[1, h], gkv[h, 0], gkv[h, 1]], axis=0)
            q = qt[h]
            s = jnp.where(hidden_keys, -1e30, score(q, tiles))
            rand_tiles = []
            rand_scores = []
            for b in range(2):
                base = (b * heads + h) * rand
                t = jnp.concatenate([recv[rtab[base + r]] for r in range(rand)], axis=0)
                rand_tiles.append(t)
                rand_scores.append(score(q[b * BLOCK:(b + 1) * BLOCK], t))
            sr = jnp.concatenate(rand_scores, axis=0)
            top = jnp.maximum(jnp.max(s, axis=1, keepdims=True), jnp.max(sr, axis=1, keepdims=True))
            e = jnp.exp(s - top)
            er = jnp.exp(sr - top)
            inv = 1.0 / (jnp.sum(e, axis=1, keepdims=True) + jnp.sum(er, axis=1, keepdims=True))
            pr = (er * inv).astype(bf16)
            ctx = jnp.dot((e * inv).astype(bf16), tiles, preferred_element_type=f32)
            ctx = ctx + jnp.concatenate(
                [jnp.dot(pr[b * BLOCK:(b + 1) * BLOCK], rand_tiles[b], preferred_element_type=f32) for b in range(2)],
                axis=0)
            results.append(ctx)
        both = jnp.where(low, results[0], results[1])
        cols = pl.ds(pl.multiple_of(p * 128, 128), 128)
        for b in range(2):
            rows = both[b * BLOCK:(b + 1) * BLOCK].astype(bf16)
            for g in range(G):
                ge = gctx[2 * p].reshape(2 * BLOCK, 128)[g * BLOCK:(g + 1) * BLOCK]
                go = gctx[2 * p + 1].reshape(2 * BLOCK, 128)[g * BLOCK:(g + 1) * BLOCK]
                rows = jnp.where(2 * me + b == gb[g], jnp.where(low_b, ge, go), rows)
            att[b * BLOCK:(b + 1) * BLOCK, cols] = rows
        return c

    lax.fori_loop(0, pairs, attend, 0)
    mixed = hidden[...].astype(f32) + jnp.dot(att[...], weight[...], preferred_element_type=f32)
    mean = jnp.mean(mixed, axis=1, keepdims=True)
    centred = mixed - mean
    var = jnp.mean(centred * centred, axis=1, keepdims=True)
    out[...] = (centred * lax.rsqrt(var + 1e-05) * gain[...]).astype(bf16)

    wait_sent(candq.at[pl.ds(0, plane - 1)], 0)
    wait_sent(candkv.at[pl.ds(0, plane - 1)], 1)
    wait_sent(zq.at[pl.ds(0, NZ - 1)], 2)
    wait_sent(gq.at[pl.ds(0, plane - 1)], 3)
    wait_sent(zkv.at[pl.ds(0, NZ - 1)], 4)
    w0.wait_send()
    w1.wait_send()
    wait_sent(gkv.at[pl.ds(0, plane - 1)], 8)
    wait_sent(zpart.at[pl.ds(0, NZ - 1)], 9)
    wait_sent(ghead.at[pl.ds(0, NZ - 1)], 10)
    wait_sent(gctx.at[pl.ds(0, plane - 1)], 11)
    pltpu.make_async_copy(recv.at[pl.ds(0, 2 * count - 2)], recv.at[pl.ds(0, 2 * count - 2)], a2a_s).wait()


def per_device(queries, keys, values, hidden, out_weight, norm_gain, random_blocks, global_blocks):
    row_count, width = queries.shape
    heads, rand = random_blocks.shape[1:]
    count, plane = NX * NY * NZ, NX * NY
    zrows = 2 * BLOCK // NZ
    vmem = pl.BlockSpec(memory_space=pltpu.VMEM)
    smem = pl.BlockSpec(memory_space=pltpu.SMEM)
    anym = pl.BlockSpec(memory_space=pl.ANY)
    shape = jax.ShapeDtypeStruct
    payload, kvt, qt, candq, candkv, rtab = pl.pallas_call(
        functools.partial(prep_kernel, heads, rand),
        out_shape=(
            shape((2 * count, BLOCK, 128), bf16),
            shape((2 * heads, BLOCK, 128), bf16),
            shape((heads, 2 * BLOCK, 128), bf16),
            shape((plane, BLOCK, 128), bf16),
            shape((heads, G, BLOCK, 128), bf16),
            shape((2 * heads * rand,), jnp.int32),
        ),
        in_specs=[vmem, vmem, vmem, vmem, smem],
        out_specs=(vmem, vmem, vmem, vmem, vmem, smem),
        scratch_shapes=[
            pltpu.VMEM((2, 2 * count), jnp.int32),
            pltpu.SMEM((2, 2 * count), jnp.int32),
            pltpu.SMEM((rand, heads, 2 * count), jnp.int32),
            pltpu.SMEM((count,), jnp.int32),
            pltpu.SemaphoreType.DMA((2,)),
        ],
        compiler_params=pltpu.CompilerParams(vmem_limit_bytes=24 << 20),
        name="prep",
    )(queries, keys, values, jnp.transpose(random_blocks, (2, 1, 0)), global_blocks)
    return pl.pallas_call(
        functools.partial(main_kernel, heads, rand),
        out_shape=shape((row_count, width), bf16),
        in_specs=[anym, vmem, vmem, vmem, vmem, vmem, vmem, vmem, smem, smem],
        out_specs=vmem,
        scratch_shapes=[
            pltpu.VMEM((2 * count, BLOCK, 128), bf16),
            pltpu.VMEM((2, heads, BLOCK, 128), bf16),
            pltpu.VMEM((plane, BLOCK, 128), bf16),
            pltpu.VMEM((NZ, BLOCK, 128), bf16),
            pltpu.VMEM((plane, BLOCK, 128), bf16),
            pltpu.VMEM((plane, G, BLOCK, 128), bf16),
            pltpu.VMEM((NZ, G, BLOCK, 128), bf16),
            pltpu.VMEM((plane, G, BLOCK, 128), bf16),
            pltpu.VMEM((heads, 2 * BLOCK, 128), f32),
            pltpu.VMEM((heads, 2 * BLOCK, 128), f32),
            pltpu.VMEM((NZ, zrows, 128), f32),
            pltpu.VMEM((NZ, zrows, 128), bf16),
            pltpu.VMEM((heads, NZ, zrows, 128), bf16),
            pltpu.VMEM((row_count, width), bf16),
            pltpu.SemaphoreType.DMA,
            pltpu.SemaphoreType.DMA,
            pltpu.SemaphoreType.DMA((12,)),
            pltpu.SemaphoreType.DMA((12,)),
            pltpu.SemaphoreType.DMA((6,)),
        ],
        compiler_params=pltpu.CompilerParams(
            collective_id=0, has_side_effects=True, vmem_limit_bytes=40 << 20),
        name="main",
    )(payload, kvt, qt, candq, candkv, hidden, out_weight, norm_gain.reshape(1, width), global_blocks, rtab)


def solution(mesh):
    placed = (
        P(("dp", "ctx"), None),
        P(("dp", "ctx"), None),
        P(("dp", "ctx"), None),
        P(("dp", "ctx"), None),
        P(),
        P(),
        P("dp", None, None),
        P("dp"),
    )
    return jax.shard_map(
        per_device, mesh=mesh, in_specs=placed, out_specs=P(("dp", "ctx"), None), check_vma=False
    )
```

```python
import functools

import jax
import jax.numpy as jnp
from jax import lax
from jax.experimental import pallas as pl
from jax.experimental.pallas import tpu as pltpu
from jax.sharding import PartitionSpec as P

BLOCK = 64
G = 2
NX, NY, NZ = 4, 4, 8
BATCHES = (10, 10, 10, 20, 12, 10, 14)
MESH = pl.DeviceIdType.MESH
bf16 = jnp.bfloat16
f32 = jnp.float32


def swap_halves(x):
    return jnp.concatenate([x[:, 64:], x[:, :64]], axis=1)


def low_half(shape):
    return lax.broadcasted_iota(jnp.int32, shape, 1) < 64


def table_kernel(heads, rand, rb, tab, rtab, tab_v, rtab_v, sem):
    count = NX * NY * NZ
    me = lax.axis_index("ctx")
    lanes = 2 * count
    first = jnp.full((1, lanes), 1e9, f32)
    last = jnp.full((1, lanes), -1.0, f32)
    lane_d = lax.broadcasted_iota(jnp.int32, (heads, lanes), 1)
    head_d = lax.broadcasted_iota(jnp.int32, (heads, lanes), 0)
    for r in range(rand):
        req = rb[r]
        mine = (req // 2) == me
        key = (((lane_d % 2) * heads + head_d) * rand + r) * 2 + req % 2
        key = key.astype(f32)
        first = jnp.minimum(first, jnp.min(jnp.where(mine, key, 1e9), axis=0, keepdims=True))
        last = jnp.maximum(last, jnp.max(jnp.where(mine, key, -1.0), axis=0, keepdims=True))
    first = jnp.minimum(first, pltpu.roll(first, lanes - 1, 1))
    last = jnp.maximum(last, pltpu.roll(last, lanes - 1, 1))

    def to_tile(key):
        key = jnp.clip(key, 0.0, float(4 * heads * rand - 1)).astype(jnp.int32)
        return (key % 2) * heads + (key // 2 // rand) % heads

    tab_v[0:1, :] = to_tile(first)
    tab_v[1:2, :] = to_tile(last)
    copy_tab = pltpu.make_async_copy(tab_v, tab, sem.at[0])
    copy_tab.start()

    pick_c = (lax.broadcasted_iota(jnp.int32, (lanes, 128), 0) == 2 * me + lax.broadcasted_iota(
        jnp.int32, (lanes, 128), 1)).astype(f32).astype(bf16)
    pick_r = (lax.broadcasted_iota(jnp.int32, (8, lanes), 1) == 2 * me + lax.broadcasted_iota(
        jnp.int32, (8, lanes), 0)).astype(f32).astype(bf16)
    pad = jnp.zeros((128 - heads, lanes), bf16)
    own_c, own_r = [], []
    for r in range(rand):
        ids = rb[r].astype(f32).astype(bf16)
        as_col = jnp.dot(ids, pick_c, preferred_element_type=f32).astype(jnp.int32) // 2
        as_row = lax.dot_general(pick_r, jnp.concatenate([ids, pad], axis=0), (((1,), (1,)), ((), ())),
                                 preferred_element_type=f32).astype(jnp.int32) // 2
        own_c.append([as_col[:, b:b + 1] for b in range(2)])
        own_r.append([as_row[b:b + 1, :] for b in range(2)])
    hc = lax.broadcasted_iota(jnp.int32, (heads, 128), 0)
    hr = lax.broadcasted_iota(jnp.int32, (heads, 128), 1)
    table = jnp.zeros((heads, 128), jnp.int32)
    for b in range(2):
        for r in range(rand):
            again = jnp.zeros((heads, 128), f32)
            for b2 in range(b + 1):
                for r2 in range(rand):
                    if b2 < b:
                        before = hr < heads
                    elif r2 < r:
                        before = hr <= hc
                    else:
                        before = hr < hc
                    same = jnp.logical_and(own_c[r][b] == own_r[r2][b2], before)
                    again = jnp.maximum(again, jnp.where(same, 1.0, 0.0))
            slot = jnp.max(again, axis=1, keepdims=True).astype(jnp.int32)
            table = jnp.where(hr == b * rand + r, own_c[r][b] * 2 + slot, table)
    rtab_v[...] = table
    copy_rtab = pltpu.make_async_copy(rtab_v, rtab, sem.at[1])
    copy_rtab.start()
    copy_tab.wait()
    copy_rtab.wait()


def main_kernel(heads, rand, queries_h, keys_h, values_h, hidden_h, weight_h, gain_h, gb, tab_s, rtab_s, out,
                queries, keys, values, hidden, weight, gain, payload, kvt, qt, qpair, candq, candkv,
                recv, win, recvq, zq, gq, recvkv, selkv, zrkv, zkv, gkv, part, rpart, zsum, zpart, ghead, gctx,
                att, early, stats, a2a_s, a2a_r, send, got, loc, load):
    count, plane = NX * NY * NZ, NX * NY
    pairs = heads // 2
    half = NZ // G
    zrows = 2 * BLOCK // NZ
    me = lax.axis_index("ctx")
    x, z, y = me % NX, (me // NX) % NZ, me // (NX * NZ)
    pos = y * NX + x

    def at(px, pz, py):
        return {"ctx": (py * NZ + pz) * NX + px}

    def shifted(k):
        kx, kz, ky = k % NX, (k // NX) % NZ, k // (NX * NZ)
        return ((y + ky) % NY * NZ + (z + kz) % NZ) * NX + (x + kx) % NX

    def remote(src, dst, s, r, device):
        return pltpu.make_async_remote_copy(
            src_ref=src, dst_ref=dst, send_sem=s, recv_sem=r, device_id=device, device_id_type=MESH)

    loads = [
        pltpu.make_async_copy(src, dst, load.at[i])
        for i, (src, dst) in enumerate((
            (queries_h, queries), (keys_h, keys), (values_h, values),
            (hidden_h, hidden), (weight_h, weight), (gain_h, gain)))
    ]
    for c in loads:
        c.start()

    barrier = pltpu.get_barrier_semaphore()

    def greet(k, c):
        pl.semaphore_signal(barrier, inc=1, device_id={"ctx": shifted(k)}, device_id_type=MESH)
        return c

    lax.fori_loop(1, count, greet, 0)

    for c in loads[:3]:
        c.wait()
    low_b = low_half((BLOCK, 128))
    for b in range(2):
        for p in range(pairs):
            qpair[b * pairs + p] = queries[b * BLOCK:(b + 1) * BLOCK, p * 128:(p + 1) * 128]
    for g in range(G):
        for p in range(pairs):
            candq[g * pairs + p] = qpair[gb[g] % 2 * pairs + p]
    for b in range(2):
        rows = slice(b * BLOCK, (b + 1) * BLOCK)
        for p in range(pairs):
            cols = slice(p * 128, (p + 1) * 128)
            kr = swap_halves(keys[rows, cols])
            vn = values[rows, cols]
            kvt[b * heads + 2 * p] = jnp.where(low_b, vn, kr)
            kvt[b * heads + 2 * p + 1] = jnp.where(low_b, kr, vn)

    def pick(h, c):
        for g in range(G):
            candkv[h, half * g:half * (g + 1)] = kvt[gb[g] % 2 * heads + h].reshape(half, BLOCK // half, 128)
        return c

    lax.fori_loop(0, heads, pick, 0)

    def fill(i, c):
        for u in range(4):
            d = 4 * i + u
            payload[2 * d] = kvt[tab_s[0, 2 * d]]
            payload[2 * d + 1] = kvt[tab_s[1, 2 * d]]
        return c

    lax.fori_loop(0, count // 4, fill, 0)
    zero_b = jnp.zeros((BLOCK, 128), bf16)
    for b in range(2):
        rows = slice(b * BLOCK, (b + 1) * BLOCK)
        for p in range(pairs):
            qr = swap_halves(queries[rows, p * 128:(p + 1) * 128])
            qt[2 * p, rows, :] = jnp.where(low_b, zero_b, qr)
            qt[2 * p + 1, rows, :] = jnp.where(low_b, qr, zero_b)
    pl.semaphore_wait(barrier, count - 1)

    issued = [1]

    def batch(n):
        lo = issued[0]
        hi = min(count, lo + n)
        issued[0] = hi

        def one(k, c):
            d = shifted((k * 37) % count)
            remote(payload.at[pl.ds(2 * d, 2)], recv.at[pl.ds(2 * me, 2)], a2a_s, a2a_r, {"ctx": d}).start()
            return c

        if hi > lo:
            lax.fori_loop(lo, hi, one, 0)

    def to_plane(fn, i):
        def one(k, c):
            p = ((y + k // NX) % NY) * NX + (x + k % NX) % NX
            src, dst = fn(p)
            remote(src, dst, send.at[i], got.at[i], at(p % NX, z, p // NX)).start()
            return c

        lax.fori_loop(1, plane, one, 0)

    def to_line(fn, i):
        def one(k, c):
            pz = (z + k) % NZ
            src, dst = fn(pz)
            remote(src, dst, send.at[i], got.at[i], at(x, pz, y)).start()
            return c

        lax.fori_loop(1, NZ, one, 0)

    def wait_got(ref, i):
        pltpu.make_async_copy(ref, ref, got.at[i]).wait()

    def wait_sent(ref, i):
        pltpu.make_async_copy(ref, ref, send.at[i]).wait()

    def owner_of(g):
        return gb[g] // 2

    def pos_of(d):
        return (d // (NX * NZ)) * NX + d % NX

    def z_of(d):
        return (d // NX) % NZ

    own = [
        pltpu.make_async_copy(candq.at[pos], recvq.at[pos], loc.at[0]),
        pltpu.make_async_copy(candkv.at[pos], recvkv.at[pos], loc.at[1]),
        pltpu.make_async_copy(payload.at[pl.ds(2 * me, 2)], recv.at[pl.ds(2 * me, 2)], loc.at[2]),
    ]
    for c in own:
        c.start()

    to_plane(lambda p: (candq.at[p], recvq.at[pos]), 0)
    to_plane(lambda p: (candkv.at[p], recvkv.at[pos]), 1)
    batch(BATCHES[0])
    own[0].wait()
    wait_got(recvq.at[pl.ds(0, plane - 1)], 0)
    my_g = pos // pairs
    q_owner = owner_of(my_g)
    zq[z] = recvq[pos_of(q_owner)]
    batch(2)
    to_line(lambda p: (zq.at[z], zq.at[z]), 2)
    batch(BATCHES[1] - 2)
    wait_got(zq.at[pl.ds(0, NZ - 1)], 2)
    gq[pos] = zq[z_of(q_owner)]
    batch(2)
    to_plane(lambda p: (gq.at[pos], gq.at[pos]), 3)
    batch(BATCHES[2] - 2)
    own[1].wait()
    wait_got(recvkv.at[pl.ds(0, plane - 1)], 1)

    for g in range(G):
        selkv[g * half:(g + 1) * half] = recvkv[pos_of(owner_of(g))][g * half:(g + 1) * half]
    own_kv = pltpu.make_async_copy(selkv.at[z], zrkv.at[z], loc.at[8])
    batch(2)
    to_line(lambda p: (selkv.at[p], zrkv.at[z]), 4)
    own_kv.start()
    nxt, prv = (me + 1) % count, (me + count - 1) % count
    w0 = remote(kvt.at[pl.ds(heads, heads)], win.at[0], send.at[5], got.at[5], {"ctx": nxt})
    w1 = remote(kvt.at[pl.ds(0, heads)], win.at[1], send.at[6], got.at[6], {"ctx": prv})
    wait_got(gq.at[pl.ds(0, plane - 1)], 3)

    lane = lax.broadcasted_iota(jnp.int32, (2 * BLOCK, 128), 1)
    low = lane < 64

    def score(q, tiles):
        return lax.dot_general(q, tiles, (((1,), (1,)), ((), ())), preferred_element_type=f32) * 0.125

    def send_part(h):
        @pl.when(h != pos)
        def _():
            remote(part.at[h], rpart.at[pos], send.at[7], got.at[7], at(h % NX, z, h // NX)).start()

    per_pair = max(1, BATCHES[3] // pairs)

    def partial(i, c):
        @pl.when(i > 0)
        def _():
            before = (pos // 2 + i) % pairs
            send_part(2 * before)
            send_part(2 * before + 1)

        p = (pos // 2 + i + 1) % pairs
        q = jnp.concatenate([gq[p], gq[pairs + p]], axis=0)
        q = swap_halves(q)
        for odd in range(2):
            h = 2 * p + odd
            tiles = jnp.concatenate([kvt[h], kvt[heads + h]], axis=0)
            mine = low if odd else jnp.logical_not(low)
            s = score(jnp.where(mine, q, jnp.zeros_like(q)), tiles)
            top = jnp.max(s, axis=1, keepdims=True)
            e = jnp.exp(s - top)
            total = jnp.sum(e, axis=1, keepdims=True)
            hi = e.astype(bf16)
            lo = (e - hi.astype(f32)).astype(bf16)
            numer = jnp.dot(hi, tiles, preferred_element_type=f32) + jnp.dot(lo, tiles, preferred_element_type=f32)
            part[h] = jnp.where(mine, jnp.where(lane % 64 < 32, total, top), numer)
        return c

    lax.fori_loop(0, pairs, partial, 0)
    batch(2)
    last_pair = pos // 2
    send_part(2 * last_pair)
    send_part(2 * last_pair + 1)
    own_part = pltpu.make_async_copy(part.at[pos], rpart.at[pos], loc.at[3])
    own_part.start()
    batch(BATCHES[3])
    w0.start()
    w1.start()
    own_kv.wait()
    wait_got(zrkv.at[pl.ds(0, NZ - 1)], 4)
    zkv[z] = zrkv[z_of(owner_of(z // half))]
    batch(2)
    to_line(lambda p: (zkv.at[z], zkv.at[z]), 12)

    odd_head = pos % 2 == 1

    def merge(ref, n, rows):
        ln = lax.broadcasted_iota(jnp.int32, (rows, 128), 1)
        side = (ln < 64) == odd_head
        is_top = jnp.logical_and(side, ln % 64 >= 32)
        terms = [ref[j] for j in range(n)]
        tops = [jnp.max(jnp.where(is_top, t, -3e38), axis=1, keepdims=True) for t in terms]
        top = functools.reduce(jnp.maximum, tops)
        acc = functools.reduce(jnp.add, [t * jnp.exp(tj - top) for t, tj in zip(terms, tops)])
        return acc, top, side, is_top, ln

    own_part.wait()
    wait_got(rpart.at[pl.ds(0, plane - 1)], 7)

    def merge_rows(i, c):
        rows = pl.ds(pl.multiple_of(i * zrows, zrows), zrows)
        acc, top, _, is_top, _ = merge(rpart.at[:, rows, :], plane, zrows)
        zsum[i] = jnp.where(is_top, top, acc)
        return c

    lax.fori_loop(0, NZ, merge_rows, 0)
    own_z = pltpu.make_async_copy(zsum.at[z], zpart.at[z], loc.at[4])
    batch(2)
    to_line(lambda p: (zsum.at[p], zpart.at[z]), 9)
    own_z.start()
    batch(BATCHES[4] - 2)
    wait_got(zkv.at[pl.ds(0, NZ - 1)], 12)
    own_gkv = pltpu.make_async_copy(zkv, gkv.at[pos], loc.at[9])
    own_gkv.start()
    to_plane(lambda p: (zkv, gkv.at[pos]), 8)
    own_z.wait()
    wait_got(zpart.at[pl.ds(0, NZ - 1)], 9)
    acc, _, side, _, ln = merge(zpart, NZ, zrows)
    total = jnp.max(jnp.where(jnp.logical_and(side, ln % 64 < 32), acc, -3e38), axis=1, keepdims=True)
    ghead[z] = (acc / total).astype(bf16)
    batch(2)
    to_line(lambda p: (ghead.at[z], ghead.at[z]), 10)
    batch(BATCHES[5] - 2)
    wait_got(ghead.at[pl.ds(0, NZ - 1)], 10)
    own_g = pltpu.make_async_copy(ghead, gctx.at[pos], loc.at[5])
    own_g.start()
    to_plane(lambda p: (ghead, gctx.at[pos]), 11)
    batch(count)
    own_gkv.wait()
    wait_got(gkv.at[pl.ds(0, plane - 1)], 8)
    w0.wait_recv()
    w1.wait_recv()

    row = lax.broadcasted_iota(jnp.int32, (2 * BLOCK, 6 * BLOCK), 0)
    col = lax.broadcasted_iota(jnp.int32, (2 * BLOCK, 6 * BLOCK), 1)
    first_rows = row < BLOCK
    is_prev = col < BLOCK
    is_next = jnp.logical_and(col >= 3 * BLOCK, col < 4 * BLOCK)
    no_prev = jnp.logical_or(jnp.logical_not(first_rows), me == 0)
    no_next = jnp.logical_or(first_rows, me == count - 1)
    hidden_keys = jnp.logical_or(jnp.logical_and(is_prev, no_prev), jnp.logical_and(is_next, no_next))
    def shared_tiles(h):
        return jnp.concatenate(
            [win[0, h], kvt[h], kvt[heads + h], win[1, h], gkv[h].reshape(2 * BLOCK, 128)], axis=0)

    def shared(p, c):
        for odd in range(2):
            h = 2 * p + odd
            s = jnp.where(hidden_keys, -1e30, score(qt[h], shared_tiles(h)))
            top = jnp.max(s, axis=1, keepdims=True)
            e = jnp.exp(s - top)
            early[h] = e
            stats[h, 0] = jnp.broadcast_to(top, (2 * BLOCK, 128))
            stats[h, 1] = jnp.broadcast_to(jnp.sum(e, axis=1, keepdims=True), (2 * BLOCK, 128))
        return c

    for p in range(pairs):
        shared(p, 0)
    own_g.wait()
    own[2].wait()
    for c in loads[3:]:
        c.wait()
    wait_got(gctx.at[pl.ds(0, plane - 1)], 11)
    pltpu.make_async_copy(recv.at[pl.ds(0, 2 * count - 2)], recv.at[pl.ds(0, 2 * count - 2)], a2a_r).wait()

    def attend(p, c):
        results = []
        for odd in range(2):
            h = 2 * p + odd
            q = qt[h]
            rand_tiles = []
            rand_scores = []
            for b in range(2):
                t = jnp.concatenate([recv[rtab_s[h, b * rand + r]] for r in range(rand)], axis=0)
                rand_tiles.append(t)
                rand_scores.append(score(q[b * BLOCK:(b + 1) * BLOCK], t))
            sr = jnp.concatenate(rand_scores, axis=0)
            cuts = [(c, min(c + 128, rand * BLOCK)) for c in range(0, rand * BLOCK, 128)]
            parts = [sr[:, lo:hi] for lo, hi in cuts]
            top_e = stats[h, 0]
            top = functools.reduce(jnp.maximum, [jnp.max(t, axis=1, keepdims=True) for t in parts] + [top_e])
            scale = jnp.exp(top_e - top)
            parts = [jnp.exp(t - top[:, :t.shape[1]]) for t in parts]
            inv = 1.0 / functools.reduce(
                jnp.add, [jnp.sum(t, axis=1, keepdims=True) for t in parts] + [stats[h, 1] * scale])
            pr = jnp.concatenate([(t * inv[:, :t.shape[1]]).astype(bf16) for t in parts], axis=1)
            ratio = scale * inv
            ps = jnp.concatenate([(early[h, :, c:c + 128] * ratio).astype(bf16) for c in range(0, 6 * BLOCK, 128)], axis=1)
            ctx = jnp.dot(ps, shared_tiles(h), preferred_element_type=f32)
            ctx = ctx + jnp.concatenate(
                [jnp.dot(pr[b * BLOCK:(b + 1) * BLOCK], rand_tiles[b], preferred_element_type=f32) for b in range(2)],
                axis=0)
            results.append(ctx)
        both = jnp.where(low, results[0], results[1])
        cols = pl.ds(pl.multiple_of(p * 128, 128), 128)
        for b in range(2):
            rows = both[b * BLOCK:(b + 1) * BLOCK].astype(bf16)
            for g in range(G):
                ge = gctx[2 * p].reshape(2 * BLOCK, 128)[g * BLOCK:(g + 1) * BLOCK]
                go = gctx[2 * p + 1].reshape(2 * BLOCK, 128)[g * BLOCK:(g + 1) * BLOCK]
                rows = jnp.where(2 * me + b == gb[g], jnp.where(low_b, ge, go), rows)
            att[b * BLOCK:(b + 1) * BLOCK, cols] = rows
        return c

    def attend_two(i, c):
        return attend(2 * i + 1, attend(2 * i, c))

    lax.fori_loop(0, pairs // 2, attend_two, 0)
    mixed = hidden[...].astype(f32) + jnp.dot(att[...], weight[...], preferred_element_type=f32)
    mean = jnp.mean(mixed, axis=1, keepdims=True)
    centred = mixed - mean
    var = jnp.mean(centred * centred, axis=1, keepdims=True)
    out[...] = (centred * lax.rsqrt(var + 1e-05) * gain[...]).astype(bf16)

    wait_sent(candq.at[pl.ds(0, plane - 1)], 0)
    wait_sent(candkv.at[pl.ds(0, plane - 1)], 1)
    wait_sent(zq.at[pl.ds(0, NZ - 1)], 2)
    wait_sent(gq.at[pl.ds(0, plane - 1)], 3)
    wait_sent(zrkv.at[pl.ds(0, NZ - 1)], 4)
    w0.wait_send()
    w1.wait_send()
    wait_sent(rpart.at[pl.ds(0, plane - 1)], 7)
    wait_sent(gkv.at[pl.ds(0, plane - 1)], 8)
    wait_sent(zpart.at[pl.ds(0, NZ - 1)], 9)
    wait_sent(ghead.at[pl.ds(0, NZ - 1)], 10)
    wait_sent(zkv.at[pl.ds(0, NZ - 1)], 12)
    wait_sent(gctx.at[pl.ds(0, plane - 1)], 11)
    pltpu.make_async_copy(recv.at[pl.ds(0, 2 * count - 2)], recv.at[pl.ds(0, 2 * count - 2)], a2a_s).wait()


def per_device(queries, keys, values, hidden, out_weight, norm_gain, random_blocks, global_blocks):
    row_count, width = queries.shape
    heads, rand = random_blocks.shape[1:]
    count, plane = NX * NY * NZ, NX * NY
    zrows = 2 * BLOCK // NZ
    vmem = pl.BlockSpec(memory_space=pltpu.VMEM)
    smem = pl.BlockSpec(memory_space=pltpu.SMEM)
    shape = jax.ShapeDtypeStruct
    hbm = pl.BlockSpec(memory_space=pltpu.HBM)
    chunk = G * BLOCK // NZ
    tab, rtab = pl.pallas_call(
        functools.partial(table_kernel, heads, rand),
        out_shape=(shape((2, 2 * count), jnp.int32), shape((heads, 128), jnp.int32)),
        in_specs=[vmem],
        out_specs=(smem, smem),
        scratch_shapes=[
            pltpu.VMEM((2, 2 * count), jnp.int32),
            pltpu.VMEM((heads, 128), jnp.int32),
            pltpu.SemaphoreType.DMA((2,)),
        ],
        name="tables",
    )(jnp.transpose(random_blocks, (2, 1, 0)))
    return pl.pallas_call(
        functools.partial(main_kernel, heads, rand),
        out_shape=shape((row_count, width), bf16),
        in_specs=[hbm] * 6 + [smem] * 3,
        out_specs=vmem,
        scratch_shapes=[
            pltpu.VMEM((row_count, width), bf16),
            pltpu.VMEM((row_count, width), bf16),
            pltpu.VMEM((row_count, width), bf16),
            pltpu.VMEM((row_count, width), bf16),
            pltpu.VMEM((width, width), bf16),
            pltpu.VMEM((1, width), f32),
            pltpu.VMEM((2 * count, BLOCK, 128), bf16),
            pltpu.VMEM((2 * heads, BLOCK, 128), bf16),
            pltpu.VMEM((heads, 2 * BLOCK, 128), bf16),
            pltpu.VMEM((heads, BLOCK, 128), bf16),
            pltpu.VMEM((plane, BLOCK, 128), bf16),
            pltpu.VMEM((heads, NZ, chunk, 128), bf16),
            pltpu.VMEM((2 * count, BLOCK, 128), bf16),
            pltpu.VMEM((2, heads, BLOCK, 128), bf16),
            pltpu.VMEM((plane, BLOCK, 128), bf16),
            pltpu.VMEM((NZ, BLOCK, 128), bf16),
            pltpu.VMEM((plane, BLOCK, 128), bf16),
            pltpu.VMEM((plane, NZ, chunk, 128), bf16),
            pltpu.VMEM((NZ, chunk, 128), bf16),
            pltpu.VMEM((NZ, chunk, 128), bf16),
            pltpu.VMEM((NZ, chunk, 128), bf16),
            pltpu.VMEM((plane, NZ, chunk, 128), bf16),
            pltpu.VMEM((heads, 2 * BLOCK, 128), f32),
            pltpu.VMEM((heads, 2 * BLOCK, 128), f32),
            pltpu.VMEM((NZ, zrows, 128), f32),
            pltpu.VMEM((NZ, zrows, 128), f32),
            pltpu.VMEM((NZ, zrows, 128), bf16),
            pltpu.VMEM((heads, NZ, zrows, 128), bf16),
            pltpu.VMEM((row_count, width), bf16),
            pltpu.VMEM((heads, 2 * BLOCK, 6 * BLOCK), f32),
            pltpu.VMEM((heads, 2, 2 * BLOCK, 128), f32),
            pltpu.SemaphoreType.DMA,
            pltpu.SemaphoreType.DMA,
            pltpu.SemaphoreType.DMA((13,)),
            pltpu.SemaphoreType.DMA((13,)),
            pltpu.SemaphoreType.DMA((10,)),
            pltpu.SemaphoreType.DMA((6,)),
        ],
        compiler_params=pltpu.CompilerParams(
            collective_id=0, has_side_effects=True, vmem_limit_bytes=67043328),
        name="main",
    )(queries, keys, values, hidden, out_weight, norm_gain.reshape(1, width),
      global_blocks, tab, rtab)


def solution(mesh):
    placed = (
        P(("dp", "ctx"), None),
        P(("dp", "ctx"), None),
        P(("dp", "ctx"), None),
        P(("dp", "ctx"), None),
        P(),
        P(),
        P("dp", None, None),
        P("dp"),
    )
    return jax.shard_map(
        per_device, mesh=mesh, in_specs=placed, out_specs=P(("dp", "ctx"), None), check_vma=False
    )
```

```python
import functools

import jax
import jax.numpy as jnp
from jax import lax
from jax.experimental import pallas as pl
from jax.experimental.pallas import tpu as pltpu
from jax.sharding import PartitionSpec as P

BLOCK = 64
G = 2
NX, NY, NZ = 4, 4, 8
BATCHES = (10, 10, 10, 20, 12, 10, 14)
MESH = pl.DeviceIdType.MESH
bf16 = jnp.bfloat16
f32 = jnp.float32


def swap_halves(x):
    return jnp.concatenate([x[:, 64:], x[:, :64]], axis=1)


def low_half(shape):
    return lax.broadcasted_iota(jnp.int32, shape, 1) < 64


def table_kernel(heads, rand, rb, tab, rtab, tab_v, rtab_v, sem):
    count = NX * NY * NZ
    me = lax.axis_index("ctx")
    lanes = 2 * count
    first = jnp.full((1, lanes), 1e9, f32)
    last = jnp.full((1, lanes), -1.0, f32)
    lane_d = lax.broadcasted_iota(jnp.int32, (heads, lanes), 1)
    head_d = lax.broadcasted_iota(jnp.int32, (heads, lanes), 0)
    for r in range(rand):
        req = rb[r]
        mine = (req // 2) == me
        key = (((lane_d % 2) * heads + head_d) * rand + r) * 2 + req % 2
        key = key.astype(f32)
        first = jnp.minimum(first, jnp.min(jnp.where(mine, key, 1e9), axis=0, keepdims=True))
        last = jnp.maximum(last, jnp.max(jnp.where(mine, key, -1.0), axis=0, keepdims=True))
    first = jnp.minimum(first, pltpu.roll(first, lanes - 1, 1))
    last = jnp.maximum(last, pltpu.roll(last, lanes - 1, 1))

    def to_tile(key):
        key = jnp.clip(key, 0.0, float(4 * heads * rand - 1)).astype(jnp.int32)
        return (key % 2) * heads + (key // 2 // rand) % heads

    tab_v[0:1, :] = to_tile(first)
    tab_v[1:2, :] = to_tile(last)
    copy_tab = pltpu.make_async_copy(tab_v, tab, sem.at[0])
    copy_tab.start()

    pick_c = (lax.broadcasted_iota(jnp.int32, (lanes, 128), 0) == 2 * me + lax.broadcasted_iota(
        jnp.int32, (lanes, 128), 1)).astype(f32).astype(bf16)
    pick_r = (lax.broadcasted_iota(jnp.int32, (8, lanes), 1) == 2 * me + lax.broadcasted_iota(
        jnp.int32, (8, lanes), 0)).astype(f32).astype(bf16)
    pad = jnp.zeros((128 - heads, lanes), bf16)
    own_c, own_r = [], []
    for r in range(rand):
        ids = rb[r].astype(f32).astype(bf16)
        as_col = jnp.dot(ids, pick_c, preferred_element_type=f32).astype(jnp.int32) // 2
        as_row = lax.dot_general(pick_r, jnp.concatenate([ids, pad], axis=0), (((1,), (1,)), ((), ())),
                                 preferred_element_type=f32).astype(jnp.int32) // 2
        own_c.append([as_col[:, b:b + 1] for b in range(2)])
        own_r.append([as_row[b:b + 1, :] for b in range(2)])
    hc = lax.broadcasted_iota(jnp.int32, (heads, 128), 0)
    hr = lax.broadcasted_iota(jnp.int32, (heads, 128), 1)
    table = jnp.zeros((heads, 128), jnp.int32)
    for b in range(2):
        for r in range(rand):
            again = jnp.zeros((heads, 128), f32)
            for b2 in range(b + 1):
                for r2 in range(rand):
                    if b2 < b:
                        before = hr < heads
                    elif r2 < r:
                        before = hr <= hc
                    else:
                        before = hr < hc
                    same = jnp.logical_and(own_c[r][b] == own_r[r2][b2], before)
                    again = jnp.maximum(again, jnp.where(same, 1.0, 0.0))
            slot = jnp.max(again, axis=1, keepdims=True).astype(jnp.int32)
            table = jnp.where(hr == b * rand + r, own_c[r][b] * 2 + slot, table)
    rtab_v[...] = table
    copy_rtab = pltpu.make_async_copy(rtab_v, rtab, sem.at[1])
    copy_rtab.start()
    copy_tab.wait()
    copy_rtab.wait()


def main_kernel(heads, rand, queries_h, keys_h, values_h, hidden_h, weight_h, gain_h, gb, tab_s, rtab_s, out,
                queries, keys, values, hidden, weight, gain, payload, kvt, qt, qpair, candq, candkv,
                recv, win, recvq, zq, gq, recvkv, selkv, zrkv, zkv, gkv, part, rpart, zsum, zpart, ghead, gctx,
                att, early, stats, a2a_s, a2a_r, send, got, loc, load):
    count, plane = NX * NY * NZ, NX * NY
    pairs = heads // 2
    half = NZ // G
    zrows = 2 * BLOCK // NZ
    me = lax.axis_index("ctx")
    x, z, y = me % NX, (me // NX) % NZ, me // (NX * NZ)
    pos = y * NX + x

    def at(px, pz, py):
        return {"ctx": (py * NZ + pz) * NX + px}

    def shifted(k):
        kx, kz, ky = k % NX, (k // NX) % NZ, k // (NX * NZ)
        return ((y + ky) % NY * NZ + (z + kz) % NZ) * NX + (x + kx) % NX

    def remote(src, dst, s, r, device):
        return pltpu.make_async_remote_copy(
            src_ref=src, dst_ref=dst, send_sem=s, recv_sem=r, device_id=device, device_id_type=MESH)

    loads = [
        pltpu.make_async_copy(src, dst, load.at[i])
        for i, (src, dst) in enumerate((
            (queries_h, queries), (keys_h, keys), (values_h, values),
            (hidden_h, hidden), (weight_h, weight), (gain_h, gain)))
    ]
    for c in loads:
        c.start()

    barrier = pltpu.get_barrier_semaphore()

    def greet(k, c):
        pl.semaphore_signal(barrier, inc=1, device_id={"ctx": shifted(k)}, device_id_type=MESH)
        return c

    lax.fori_loop(1, count, greet, 0)

    for c in loads[:3]:
        c.wait()
    low_b = low_half((BLOCK, 128))
    for b in range(2):
        for p in range(pairs):
            qpair[b * pairs + p] = queries[b * BLOCK:(b + 1) * BLOCK, p * 128:(p + 1) * 128]
    for g in range(G):
        for p in range(pairs):
            candq[g * pairs + p] = qpair[gb[g] % 2 * pairs + p]
    for b in range(2):
        rows = slice(b * BLOCK, (b + 1) * BLOCK)
        for p in range(pairs):
            cols = slice(p * 128, (p + 1) * 128)
            kr = swap_halves(keys[rows, cols])
            vn = values[rows, cols]
            kvt[b * heads + 2 * p] = jnp.where(low_b, vn, kr)
            kvt[b * heads + 2 * p + 1] = jnp.where(low_b, kr, vn)

    def pick(h, c):
        for g in range(G):
            candkv[h, half * g:half * (g + 1)] = kvt[gb[g] % 2 * heads + h].reshape(half, BLOCK // half, 128)
        return c

    lax.fori_loop(0, heads, pick, 0)

    def fill(i, c):
        for u in range(4):
            d = 4 * i + u
            payload[2 * d] = kvt[tab_s[0, 2 * d]]
            payload[2 * d + 1] = kvt[tab_s[1, 2 * d]]
        return c

    lax.fori_loop(0, count // 4, fill, 0)
    pl.semaphore_wait(barrier, count - 1)

    issued = [1]

    def batch(n):
        lo = issued[0]
        hi = min(count, lo + n)
        issued[0] = hi

        def one(k, c):
            d = shifted((k * 37) % count)
            remote(payload.at[pl.ds(2 * d, 2)], recv.at[pl.ds(2 * me, 2)], a2a_s, a2a_r, {"ctx": d}).start()
            return c

        if hi > lo:
            lax.fori_loop(lo, hi, one, 0)

    def to_plane(fn, i):
        def one(k, c):
            p = ((y + k // NX) % NY) * NX + (x + k % NX) % NX
            src, dst = fn(p)
            remote(src, dst, send.at[i], got.at[i], at(p % NX, z, p // NX)).start()
            return c

        lax.fori_loop(1, plane, one, 0)

    def to_line(fn, i):
        def one(k, c):
            pz = (z + k) % NZ
            src, dst = fn(pz)
            remote(src, dst, send.at[i], got.at[i], at(x, pz, y)).start()
            return c

        lax.fori_loop(1, NZ, one, 0)

    def wait_got(ref, i):
        pltpu.make_async_copy(ref, ref, got.at[i]).wait()

    def wait_sent(ref, i):
        pltpu.make_async_copy(ref, ref, send.at[i]).wait()

    def owner_of(g):
        return gb[g] // 2

    def pos_of(d):
        return (d // (NX * NZ)) * NX + d % NX

    def z_of(d):
        return (d // NX) % NZ

    own = [
        pltpu.make_async_copy(candq.at[pos], recvq.at[pos], loc.at[0]),
        pltpu.make_async_copy(candkv.at[pos], recvkv.at[pos], loc.at[1]),
        pltpu.make_async_copy(payload.at[pl.ds(2 * me, 2)], recv.at[pl.ds(2 * me, 2)], loc.at[2]),
    ]
    for c in own:
        c.start()

    to_plane(lambda p: (candq.at[p], recvq.at[pos]), 0)
    to_plane(lambda p: (candkv.at[p], recvkv.at[pos]), 1)
    batch(BATCHES[0])
    zero_b = jnp.zeros((BLOCK, 128), bf16)
    for b in range(2):
        rows = slice(b * BLOCK, (b + 1) * BLOCK)
        for p in range(pairs):
            qr = swap_halves(queries[rows, p * 128:(p + 1) * 128])
            qt[2 * p, rows, :] = jnp.where(low_b, zero_b, qr)
            qt[2 * p + 1, rows, :] = jnp.where(low_b, qr, zero_b)
    own[0].wait()
    wait_got(recvq.at[pl.ds(0, plane - 1)], 0)
    my_g = pos // pairs
    q_owner = owner_of(my_g)
    zq[z] = recvq[pos_of(q_owner)]
    batch(2)
    to_line(lambda p: (zq.at[z], zq.at[z]), 2)
    batch(BATCHES[1] - 2)
    wait_got(zq.at[pl.ds(0, NZ - 1)], 2)
    gq[pos] = zq[z_of(q_owner)]
    batch(2)
    to_plane(lambda p: (gq.at[pos], gq.at[pos]), 3)
    batch(BATCHES[2] - 2)
    own[1].wait()
    wait_got(recvkv.at[pl.ds(0, plane - 1)], 1)

    for g in range(G):
        selkv[g * half:(g + 1) * half] = recvkv[pos_of(owner_of(g))][g * half:(g + 1) * half]
    own_kv = pltpu.make_async_copy(selkv.at[z], zrkv.at[z], loc.at[8])
    batch(2)
    to_line(lambda p: (selkv.at[p], zrkv.at[z]), 4)
    own_kv.start()
    nxt, prv = (me + 1) % count, (me + count - 1) % count
    w0 = remote(kvt.at[pl.ds(heads, heads)], win.at[0], send.at[5], got.at[5], {"ctx": nxt})
    w1 = remote(kvt.at[pl.ds(0, heads)], win.at[1], send.at[6], got.at[6], {"ctx": prv})
    wait_got(gq.at[pl.ds(0, plane - 1)], 3)

    lane = lax.broadcasted_iota(jnp.int32, (2 * BLOCK, 128), 1)
    low = lane < 64

    def score(q, tiles):
        return lax.dot_general(q, tiles, (((1,), (1,)), ((), ())), preferred_element_type=f32) * 0.125

    def send_part(h):
        @pl.when(h != pos)
        def _():
            remote(part.at[h], rpart.at[pos], send.at[7], got.at[7], at(h % NX, z, h // NX)).start()

    per_pair = max(1, BATCHES[3] // pairs)

    def partial(i, c):
        @pl.when(i > 0)
        def _():
            before = (pos // 2 + i) % pairs
            send_part(2 * before)
            send_part(2 * before + 1)

        p = (pos // 2 + i + 1) % pairs
        q = jnp.concatenate([gq[p], gq[pairs + p]], axis=0)
        q = swap_halves(q)
        for odd in range(2):
            h = 2 * p + odd
            tiles = jnp.concatenate([kvt[h], kvt[heads + h]], axis=0)
            mine = low if odd else jnp.logical_not(low)
            s = score(jnp.where(mine, q, jnp.zeros_like(q)), tiles)
            top = jnp.max(s, axis=1, keepdims=True)
            e = jnp.exp(s - top)
            total = jnp.sum(e, axis=1, keepdims=True)
            hi = e.astype(bf16)
            lo = (e - hi.astype(f32)).astype(bf16)
            numer = jnp.dot(hi, tiles, preferred_element_type=f32) + jnp.dot(lo, tiles, preferred_element_type=f32)
            part[h] = jnp.where(mine, jnp.where(lane % 64 < 32, total, top), numer)
        return c

    for i in range(pairs):
        partial(i, 0)
    batch(2)
    last_pair = pos // 2
    send_part(2 * last_pair)
    send_part(2 * last_pair + 1)
    own_part = pltpu.make_async_copy(part.at[pos], rpart.at[pos], loc.at[3])
    own_part.start()
    batch(BATCHES[3])
    w0.start()
    w1.start()
    own_kv.wait()
    wait_got(zrkv.at[pl.ds(0, NZ - 1)], 4)
    zkv[z] = zrkv[z_of(owner_of(z // half))]
    batch(2)
    to_line(lambda p: (zkv.at[z], zkv.at[z]), 12)

    odd_head = pos % 2 == 1

    def merge(ref, n, rows):
        ln = lax.broadcasted_iota(jnp.int32, (rows, 128), 1)
        side = (ln < 64) == odd_head
        is_top = jnp.logical_and(side, ln % 64 >= 32)
        terms = [ref[j] for j in range(n)]
        tops = [jnp.max(jnp.where(is_top, t, -3e38), axis=1, keepdims=True) for t in terms]
        top = functools.reduce(jnp.maximum, tops)
        acc = functools.reduce(jnp.add, [t * jnp.exp(tj - top) for t, tj in zip(terms, tops)])
        return acc, top, side, is_top, ln

    own_part.wait()
    wait_got(rpart.at[pl.ds(0, plane - 1)], 7)

    def merge_rows(i, c):
        rows = pl.ds(pl.multiple_of(i * zrows, zrows), zrows)
        acc, top, _, is_top, _ = merge(rpart.at[:, rows, :], plane, zrows)
        zsum[i] = jnp.where(is_top, top, acc)
        return c

    lax.fori_loop(0, NZ, merge_rows, 0)
    own_z = pltpu.make_async_copy(zsum.at[z], zpart.at[z], loc.at[4])
    batch(2)
    to_line(lambda p: (zsum.at[p], zpart.at[z]), 9)
    own_z.start()
    batch(BATCHES[4] - 2)
    wait_got(zkv.at[pl.ds(0, NZ - 1)], 12)
    own_gkv = pltpu.make_async_copy(zkv, gkv.at[pos], loc.at[9])
    own_gkv.start()
    to_plane(lambda p: (zkv, gkv.at[pos]), 8)
    own_z.wait()
    wait_got(zpart.at[pl.ds(0, NZ - 1)], 9)
    acc, _, side, _, ln = merge(zpart, NZ, zrows)
    total = jnp.max(jnp.where(jnp.logical_and(side, ln % 64 < 32), acc, -3e38), axis=1, keepdims=True)
    ghead[z] = (acc / total).astype(bf16)
    batch(2)
    to_line(lambda p: (ghead.at[z], ghead.at[z]), 10)
    batch(BATCHES[5] - 2)
    wait_got(ghead.at[pl.ds(0, NZ - 1)], 10)
    own_g = pltpu.make_async_copy(ghead, gctx.at[pos], loc.at[5])
    own_g.start()
    to_plane(lambda p: (ghead, gctx.at[pos]), 11)
    batch(count)
    own_gkv.wait()
    wait_got(gkv.at[pl.ds(0, plane - 1)], 8)
    w0.wait_recv()
    w1.wait_recv()

    row = lax.broadcasted_iota(jnp.int32, (2 * BLOCK, 6 * BLOCK), 0)
    col = lax.broadcasted_iota(jnp.int32, (2 * BLOCK, 6 * BLOCK), 1)
    first_rows = row < BLOCK
    is_prev = col < BLOCK
    is_next = jnp.logical_and(col >= 3 * BLOCK, col < 4 * BLOCK)
    no_prev = jnp.logical_or(jnp.logical_not(first_rows), me == 0)
    no_next = jnp.logical_or(first_rows, me == count - 1)
    hidden_keys = jnp.logical_or(jnp.logical_and(is_prev, no_prev), jnp.logical_and(is_next, no_next))
    def shared_tiles(h):
        return jnp.concatenate(
            [win[0, h], kvt[h], kvt[heads + h], win[1, h], gkv[h].reshape(2 * BLOCK, 128)], axis=0)

    def shared(p, c):
        for odd in range(2):
            h = 2 * p + odd
            s = jnp.where(hidden_keys, -1e30, score(qt[h], shared_tiles(h)))
            top = jnp.max(s, axis=1, keepdims=True)
            e = jnp.exp(s - top)
            early[h] = e
            stats[h, 0] = jnp.broadcast_to(top, (2 * BLOCK, 128))
            stats[h, 1] = jnp.broadcast_to(jnp.sum(e, axis=1, keepdims=True), (2 * BLOCK, 128))
        return c

    for p in range(pairs):
        shared(p, 0)
    own_g.wait()
    own[2].wait()
    for c in loads[3:]:
        c.wait()
    wait_got(gctx.at[pl.ds(0, plane - 1)], 11)
    pltpu.make_async_copy(recv.at[pl.ds(0, 2 * count - 2)], recv.at[pl.ds(0, 2 * count - 2)], a2a_r).wait()

    def attend(p, c):
        results = []
        for odd in range(2):
            h = 2 * p + odd
            q = qt[h]
            rand_tiles = []
            rand_scores = []
            for b in range(2):
                t = jnp.concatenate([recv[rtab_s[h, b * rand + r]] for r in range(rand)], axis=0)
                rand_tiles.append(t)
                rand_scores.append(score(q[b * BLOCK:(b + 1) * BLOCK], t))
            sr = jnp.concatenate(rand_scores, axis=0)
            cuts = [(c, min(c + 128, rand * BLOCK)) for c in range(0, rand * BLOCK, 128)]
            parts = [sr[:, lo:hi] for lo, hi in cuts]
            top_e = stats[h, 0]
            top = functools.reduce(jnp.maximum, [jnp.max(t, axis=1, keepdims=True) for t in parts] + [top_e])
            scale = jnp.exp(top_e - top)
            parts = [jnp.exp(t - top[:, :t.shape[1]]) for t in parts]
            inv = 1.0 / functools.reduce(
                jnp.add, [jnp.sum(t, axis=1, keepdims=True) for t in parts] + [stats[h, 1] * scale])
            pr = jnp.concatenate([(t * inv[:, :t.shape[1]]).astype(bf16) for t in parts], axis=1)
            ratio = scale * inv
            ps = jnp.concatenate([(early[h, :, c:c + 128] * ratio).astype(bf16) for c in range(0, 6 * BLOCK, 128)], axis=1)
            ctx = jnp.dot(ps, shared_tiles(h), preferred_element_type=f32)
            ctx = ctx + jnp.concatenate(
                [jnp.dot(pr[b * BLOCK:(b + 1) * BLOCK], rand_tiles[b], preferred_element_type=f32) for b in range(2)],
                axis=0)
            results.append(ctx)
        both = jnp.where(low, results[0], results[1])
        cols = pl.ds(pl.multiple_of(p * 128, 128), 128)
        for b in range(2):
            rows = both[b * BLOCK:(b + 1) * BLOCK].astype(bf16)
            for g in range(G):
                ge = gctx[2 * p].reshape(2 * BLOCK, 128)[g * BLOCK:(g + 1) * BLOCK]
                go = gctx[2 * p + 1].reshape(2 * BLOCK, 128)[g * BLOCK:(g + 1) * BLOCK]
                rows = jnp.where(2 * me + b == gb[g], jnp.where(low_b, ge, go), rows)
            att[b * BLOCK:(b + 1) * BLOCK, cols] = rows
        return c

    def attend_two(i, c):
        return attend(2 * i + 1, attend(2 * i, c))

    lax.fori_loop(0, pairs // 2, attend_two, 0)
    mixed = hidden[...].astype(f32) + jnp.dot(att[...], weight[...], preferred_element_type=f32)
    mean = jnp.mean(mixed, axis=1, keepdims=True)
    centred = mixed - mean
    var = jnp.mean(centred * centred, axis=1, keepdims=True)
    out[...] = (centred * lax.rsqrt(var + 1e-05) * gain[...]).astype(bf16)

    wait_sent(candq.at[pl.ds(0, plane - 1)], 0)
    wait_sent(candkv.at[pl.ds(0, plane - 1)], 1)
    wait_sent(zq.at[pl.ds(0, NZ - 1)], 2)
    wait_sent(gq.at[pl.ds(0, plane - 1)], 3)
    wait_sent(zrkv.at[pl.ds(0, NZ - 1)], 4)
    w0.wait_send()
    w1.wait_send()
    wait_sent(rpart.at[pl.ds(0, plane - 1)], 7)
    wait_sent(gkv.at[pl.ds(0, plane - 1)], 8)
    wait_sent(zpart.at[pl.ds(0, NZ - 1)], 9)
    wait_sent(ghead.at[pl.ds(0, NZ - 1)], 10)
    wait_sent(zkv.at[pl.ds(0, NZ - 1)], 12)
    wait_sent(gctx.at[pl.ds(0, plane - 1)], 11)
    pltpu.make_async_copy(recv.at[pl.ds(0, 2 * count - 2)], recv.at[pl.ds(0, 2 * count - 2)], a2a_s).wait()


def per_device(queries, keys, values, hidden, out_weight, norm_gain, random_blocks, global_blocks):
    row_count, width = queries.shape
    heads, rand = random_blocks.shape[1:]
    count, plane = NX * NY * NZ, NX * NY
    zrows = 2 * BLOCK // NZ
    vmem = pl.BlockSpec(memory_space=pltpu.VMEM)
    smem = pl.BlockSpec(memory_space=pltpu.SMEM)
    shape = jax.ShapeDtypeStruct
    hbm = pl.BlockSpec(memory_space=pltpu.HBM)
    chunk = G * BLOCK // NZ
    tab, rtab = pl.pallas_call(
        functools.partial(table_kernel, heads, rand),
        out_shape=(shape((2, 2 * count), jnp.int32), shape((heads, 128), jnp.int32)),
        in_specs=[vmem],
        out_specs=(smem, smem),
        scratch_shapes=[
            pltpu.VMEM((2, 2 * count), jnp.int32),
            pltpu.VMEM((heads, 128), jnp.int32),
            pltpu.SemaphoreType.DMA((2,)),
        ],
        name="tables",
    )(jnp.transpose(random_blocks, (2, 1, 0)))
    return pl.pallas_call(
        functools.partial(main_kernel, heads, rand),
        out_shape=shape((row_count, width), bf16),
        in_specs=[hbm] * 6 + [smem] * 3,
        out_specs=vmem,
        scratch_shapes=[
            pltpu.VMEM((row_count, width), bf16),
            pltpu.VMEM((row_count, width), bf16),
            pltpu.VMEM((row_count, width), bf16),
            pltpu.VMEM((row_count, width), bf16),
            pltpu.VMEM((width, width), bf16),
            pltpu.VMEM((1, width), f32),
            pltpu.VMEM((2 * count, BLOCK, 128), bf16),
            pltpu.VMEM((2 * heads, BLOCK, 128), bf16),
            pltpu.VMEM((heads, 2 * BLOCK, 128), bf16),
            pltpu.VMEM((heads, BLOCK, 128), bf16),
            pltpu.VMEM((plane, BLOCK, 128), bf16),
            pltpu.VMEM((heads, NZ, chunk, 128), bf16),
            pltpu.VMEM((2 * count, BLOCK, 128), bf16),
            pltpu.VMEM((2, heads, BLOCK, 128), bf16),
            pltpu.VMEM((plane, BLOCK, 128), bf16),
            pltpu.VMEM((NZ, BLOCK, 128), bf16),
            pltpu.VMEM((plane, BLOCK, 128), bf16),
            pltpu.VMEM((plane, NZ, chunk, 128), bf16),
            pltpu.VMEM((NZ, chunk, 128), bf16),
            pltpu.VMEM((NZ, chunk, 128), bf16),
            pltpu.VMEM((NZ, chunk, 128), bf16),
            pltpu.VMEM((plane, NZ, chunk, 128), bf16),
            pltpu.VMEM((heads, 2 * BLOCK, 128), f32),
            pltpu.VMEM((heads, 2 * BLOCK, 128), f32),
            pltpu.VMEM((NZ, zrows, 128), f32),
            pltpu.VMEM((NZ, zrows, 128), f32),
            pltpu.VMEM((NZ, zrows, 128), bf16),
            pltpu.VMEM((heads, NZ, zrows, 128), bf16),
            pltpu.VMEM((row_count, width), bf16),
            pltpu.VMEM((heads, 2 * BLOCK, 6 * BLOCK), f32),
            pltpu.VMEM((heads, 2, 2 * BLOCK, 128), f32),
            pltpu.SemaphoreType.DMA,
            pltpu.SemaphoreType.DMA,
            pltpu.SemaphoreType.DMA((13,)),
            pltpu.SemaphoreType.DMA((13,)),
            pltpu.SemaphoreType.DMA((10,)),
            pltpu.SemaphoreType.DMA((6,)),
        ],
        compiler_params=pltpu.CompilerParams(
            collective_id=0, has_side_effects=True, vmem_limit_bytes=67043328),
        name="main",
    )(queries, keys, values, hidden, out_weight, norm_gain.reshape(1, width),
      global_blocks, tab, rtab)


def solution(mesh):
    placed = (
        P(("dp", "ctx"), None),
        P(("dp", "ctx"), None),
        P(("dp", "ctx"), None),
        P(("dp", "ctx"), None),
        P(),
        P(),
        P("dp", None, None),
        P("dp"),
    )
    return jax.shard_map(
        per_device, mesh=mesh, in_specs=placed, out_specs=P(("dp", "ctx"), None), check_vma=False
    )
```
